256 devices in a mesh: tile: 16 (over z, core), offs: 16 (over x, y).
Axes of the slice: x: 4, y: 4, z: 8, core: 2. Of those that a mesh axis runs over, the one named last changes fastest.
Arguments:
- traces: float32 [16, 128, 2, 2000], P('offs', 'tile'), may hold values from -6 to 6
- src_node: int32 [16, 128], P('offs', 'tile'), may hold values from 0 to 31
- rec_node: int32 [16, 128, 2], P('offs', 'tile'), may hold values from 0 to 31
- aperture: int32 [16, 128, 2], P('offs', 'tile'), may hold values from 0 to 15, all different within a row; in each aligned block of 8 rows (0 to 7, 8 to 15, ..., all dimensions but the last counted through in order) at most 2 rows name the same one
- time_table: int32 [32, 16, 2048], P(None, 'tile'), may hold values from 0 to 999
- amp_table: float32 [32, 16, 2048], P(None, 'tile'), may hold values from 0.05 to 0.5
- width_table: int32 [32, 16, 2048], P(None, 'tile'), may hold values from 0 to 2
Outputs:
- gathers: float32 [16, 16, 16, 128], P('tile', 'offs')
The draws below stay inside these ranges and needn't reach their ends.
Inputs may be any that keep to these rules, and one draw needn't show every extreme that they name: `aperture`: each row names 2 different image tiles. Among the 8 rows of one device (aligned blocks of rows in the order offset class, block), no tile is named more than 2 times, a bound that some block reaches.
All inputs are finite; a program needn't handle non-finite values.
Results may differ from the reference program's by a relative error of at most 0.0003.
Values sent between devices are 32-bit elements; how exact they have to be, the bound alone decides.
A program may use at most 64 MiB of HBM per device.

```python
import math
import jax
import jax.numpy as jnp
import numpy as np
from jax import lax

NT = 2000
TB = 2
BLK_DEV = 8
APER = 2
NODES = 32
CELLS = 128
DEPTH = 16
CAP = 2
NTILE = 16
NOFF = 16
BT = 128
PTS = 2048


def place_ends(values, rng, least, high):
    longest = values.shape.index(max(values.shape))
    spots = []
    for shift in (0, 1):
        where = [jax.random.randint(jax.random.fold_in(rng, axis), (), 0, length) for axis, length in enumerate(values.shape)]
        where[longest] = (where[longest] + shift) % values.shape[longest]
        spots.append(tuple(where))
    return values.at[spots[0]].set(least).at[spots[1]].set(high)


def levels(rng, shape, cuts, least, top_value):
    gain = 1.0
    for position, blocks in cuts:
        draws = jax.random.uniform(jax.random.fold_in(jax.random.fold_in(rng, 6), position), (blocks,), jnp.float32, least / len(cuts), top_value / len(cuts))
        gain = gain * jnp.repeat(jnp.exp(draws), shape[position] // blocks).reshape((-1,) + (1,) * (len(shape) - 1 - position))
    return gain


def routed_block(rng, own, number, rows, number_of, top, most, skew):
    sequence = jax.random.permutation(rng, number_of)
    crowded, common = shares(number_of, rows * top, most, skew, True), shares(number_of, rows * top, most, skew, False)
    places = jnp.arange(number_of)

    def named(tallies, offset_by):
        used = int((tallies > 0).sum())
        fixed = max(1, used // 4)
        shifted = fixed + (places - fixed + offset_by * (used - fixed)) % max(1, number_of - fixed)
        return jnp.zeros((number_of,), jnp.int32).at[sequence[jnp.where(places < fixed, places, shifted)]].set(jnp.asarray(tallies, jnp.int32))

    tallies = jnp.where(number % 4 == 0, named(crowded, number // 4), named(common, number - number // 4 - 1))
    mixed = jax.random.permutation(jax.random.fold_in(own, 3), number_of)
    source_of, sink = mixed[0:number_of // 2 * 2:2], mixed[1:number_of // 2 * 2:2]
    margin = jnp.minimum(tallies[source_of] - 1, most - tallies[sink]) // 2
    margin = jnp.where((source_of == sequence[0]) | (sink == sequence[0]) | (tallies[sink] == 0), 0, jnp.maximum(margin, 0))
    shifted = jax.random.randint(jax.random.fold_in(own, 4), (number_of // 2,), 0, 1 << 20) % (margin + 1)
    tallies = tallies.at[source_of].add(-shifted).at[sink].add(shifted)
    items = jnp.searchsorted(jnp.cumsum(tallies), jnp.arange(rows * top), side="right").astype(jnp.int32)
    table = items.reshape(top, rows).T
    table = table[jax.random.permutation(jax.random.fold_in(own, 1), rows)]
    offset_by = jax.random.randint(jax.random.fold_in(own, 2), (rows, 1), 0, top)
    return jnp.take_along_axis(table, (jnp.arange(top)[None, :] + offset_by) % top, axis=1)


def shares(amount, total, bound, slope, full):
    portions = [(1 << 20) // math.isqrt(rank ** slope) + 1 for rank in range(1, amount + 1)]
    largest = bound if full else min(bound, max(-(-total // amount), total * portions[0] // sum(portions)))
    least = 1 if total - largest >= amount - 1 else 0
    given, surplus = [largest] + [least] * (amount - 1), total - largest - least * (amount - 1)
    while surplus > 0:
        movable = [i for i in range(1, amount) if given[i] < largest] or [i for i in range(1, amount) if given[i] < bound]
        whole, left = sum([portions[i] for i in movable]), surplus
        for i in movable:
            extra = min(bound - given[i], max(1, left * portions[i] // whole), surplus)
            given[i] = given[i] + extra
            surplus = surplus - extra
    return np.array(given)


def gaussian(stream_key, dims, scale, most, split=(), held_as=jnp.bfloat16):
    array = jax.random.normal(stream_key, dims, jnp.float32) * scale
    if len(split) > 0:
        array = levels(stream_key, dims, split, -0.22, 0.18) * array
    return jnp.clip(array, min=-most, max=most).astype(held_as)


def setup_inputs(seed: int = 0) -> dict:
    seeds = jax.random.split(jax.random.key(seed), 8)
    traces = gaussian(seeds[0], (NOFF, BT, TB, NT), 1.0, 6.0, ((0, 16), (1, 16)), jnp.float32)
    src_node = place_ends(jax.random.randint(seeds[1], (NOFF, BT), 0, NODES), jax.random.fold_in(seeds[1], 1), 0, NODES - 1).astype(jnp.int32)
    rec_node = place_ends(jax.random.randint(seeds[2], (NOFF, BT, TB), 0, NODES), jax.random.fold_in(seeds[2], 1), 0, NODES - 1).astype(jnp.int32)
    aperture_keys = jax.random.split(jax.random.fold_in(seeds[3], 1), NOFF * BT // BLK_DEV)
    aperture_turns = jax.random.permutation(jax.random.fold_in(seeds[3], 3), NOFF * BT // BLK_DEV)
    aperture = jax.vmap(lambda own, number: routed_block(jax.random.fold_in(seeds[3], 2), own, number, BLK_DEV, NTILE, APER, CAP, 2))(aperture_keys, aperture_turns).reshape((NOFF, BT, APER))
    time_table = place_ends(jax.random.randint(seeds[4], (NODES, NTILE, PTS), 0, NT // 2), jax.random.fold_in(seeds[4], 1), 0, (NT // 2) - 1).astype(jnp.int32)
    amp_table = jnp.clip(jnp.exp(math.log(0.5) - 2.3025851 * jax.random.uniform(seeds[5], (NODES, NTILE, PTS), jnp.float32) ** levels(seeds[5], (NODES, NTILE, PTS), ((1, 16),), -0.2, 0.2)), 0.05, 0.5)
    width_table = place_ends(jax.random.randint(seeds[6], (NODES, NTILE, PTS), 0, 3), jax.random.fold_in(seeds[6], 1), 0, 2).astype(jnp.int32)
    return dict(traces=traces, src_node=src_node, rec_node=rec_node, aperture=aperture, time_table=time_table, amp_table=amp_table, width_table=width_table)


HALF_WIDTHS = (1, 2, 4)


def triangle(signal):
    length = signal.shape[-1]
    last_axis = signal.ndim - 1
    layers = []
    for halfwidth in HALF_WIDTHS:
        padded = jnp.pad(signal, [(0, 0)] * last_axis + [(halfwidth, halfwidth)])
        summed = jnp.zeros(signal.shape, signal.dtype)
        for offset in range(-halfwidth, halfwidth + 1):
            factor = float(halfwidth + 1 - abs(offset)) / float((halfwidth + 1) ** 2)
            summed = summed + factor * lax.slice_in_dim(padded, halfwidth + offset, halfwidth + offset + length, axis=last_axis)
        layers.append(summed)
    return jnp.stack(layers, axis=-2)


def spread(filtered, sources, receivers, live, time_rows, amp_rows, width_rows):
    samples = filtered.shape[-1]
    source_time = jnp.take(time_rows, sources, axis=0)[:, None, :]
    index_time = source_time + jnp.take(time_rows, receivers, axis=0)
    width_class = jnp.maximum(jnp.take(width_rows, sources, axis=0)[:, None, :], jnp.take(width_rows, receivers, axis=0))
    weight = jnp.take(amp_rows, sources, axis=0)[:, None, :] * jnp.take(amp_rows, receivers, axis=0) * live[:, None, None]
    flat = filtered.reshape(filtered.shape[0] * filtered.shape[1], -1)
    column = (width_class * samples + index_time).reshape(flat.shape[0], -1).astype(jnp.int32)
    picked = jnp.take_along_axis(flat, column, axis=1)
    return jnp.sum(weight.reshape(picked.shape) * picked, axis=0)


def reference(traces, src_node, rec_node, aperture, time_table, amp_table, width_table):
    classes = traces.shape[0]
    blocks = traces.shape[1]
    points = time_table.shape[2]
    image = jnp.zeros((classes, NTILE, points), traces.dtype)
    signals = traces.reshape(classes * blocks, TB, NT)
    sources = src_node.reshape(classes * blocks)
    receivers = rec_node.reshape(classes * blocks, TB)
    targets = aperture.reshape(classes * blocks, APER)
    row_ids = jnp.arange(classes * blocks, dtype=jnp.int32)

    def advance(image, inputs):
        signal, source, receiver_ids, target_ids, row = inputs
        filtered = triangle(signal)[None]
        offset_class = (row // blocks).astype(jnp.int32)
        ones = jnp.ones((1,), traces.dtype)
        for entry in range(APER):
            target = target_ids[entry].astype(jnp.int32)
            time_rows = lax.dynamic_index_in_dim(time_table, target, axis=1, keepdims=False)
            amp_rows = lax.dynamic_index_in_dim(amp_table, target, axis=1, keepdims=False)
            width_rows = lax.dynamic_index_in_dim(width_table, target, axis=1, keepdims=False)
            contribution = spread(filtered, source[None], receiver_ids[None], ones, time_rows, amp_rows, width_rows)
            current = lax.dynamic_slice(image, (offset_class, target, jnp.int32(0)), (1, 1, points))
            image = lax.dynamic_update_slice(image, current + contribution[None, None], (offset_class, target, jnp.int32(0)))
        return image, None

    image, _ = lax.scan(advance, image, (signals, sources, receivers, targets, row_ids))
    return image.reshape(classes, NTILE, DEPTH, CELLS).transpose(1, 2, 0, 3)
```

```python
import functools

import jax
import jax.numpy as jnp
from jax import lax
from jax.experimental import pallas as pl
from jax.experimental.pallas import tpu as pltpu
from jax.sharding import PartitionSpec as P

CELLS = 128
DEPTH = 16
ROWS = 16
HALF_WIDTHS = (1, 2, 4)
CLASSES = len(HALF_WIDTHS)


def shifted(x, lane, k):
    if k > 0:
        return pltpu.roll(jnp.where(lane < k, pltpu.roll(x, ROWS - 1, 0), x), 128 - k, 1)
    return pltpu.roll(jnp.where(lane >= 128 + k, pltpu.roll(x, 1, 0), x), -k, 1)


def migrate(blocks, meta, traces, times, amps, widths, image, filtered):
    tile = lax.axis_index("tile")
    lane = lax.broadcasted_iota(jnp.int32, (ROWS, 128), 1)
    image[...] = jnp.zeros_like(image)

    def block(b, carry):
        @pl.when((meta[b, 3] == tile) | (meta[b, 4] == tile))
        def _():
            source = meta[b, 0]
            source_time, source_amp, source_width = times[source], amps[source], widths[source]
            for i in range(2):
                x = traces[b, i]
                pairs = [shifted(x, lane, k) + shifted(x, lane, -k) for k in range(1, 5)]
                for c, h in enumerate(HALF_WIDTHS):
                    total = (h + 1) * x
                    for k in range(1, h + 1):
                        total += (h + 1 - k) * pairs[k - 1]
                    filtered[i, pl.ds(c * ROWS, ROWS)] = total * (1.0 / (h + 1) ** 2)
            for i in range(2):
                receiver = meta[b, 1 + i]
                sample = source_time + times[receiver]
                weight = source_amp * amps[receiver]
                row = jnp.maximum(source_width, widths[receiver]) * ROWS + (sample >> 7)
                column = sample & 127
                for z in (0, 8):
                    picked = jnp.zeros((8, 128), jnp.float32)
                    for r in range(CLASSES * ROWS):
                        values = jnp.broadcast_to(filtered[i, pl.ds(r, 1)], (8, 128))
                        values = jnp.take_along_axis(
                            values, column[z : z + 8], axis=1, mode="promise_in_bounds"
                        )
                        picked = jnp.where(row[z : z + 8] == r, values, picked)
                    image[pl.ds(z, 8)] += weight[z : z + 8] * picked

        return carry

    lax.fori_loop(0, blocks, block, 0)


def body(traces, src_node, rec_node, aperture, time_table, amp_table, width_table):
    signal = jnp.pad(traces[0], ((0, 0), (0, 0), (0, ROWS * 128 - traces.shape[3])))
    signal = signal.reshape(signal.shape[0], signal.shape[1], ROWS, 128)
    signal = lax.all_gather(signal, "tile", axis=0, tiled=True)
    meta = jnp.concatenate([src_node[0][:, None], rec_node[0], aperture[0]], axis=1)
    meta = lax.all_gather(meta, "tile", axis=0, tiled=True)
    nodes = time_table.shape[0]
    tables = [t.reshape(nodes, DEPTH, CELLS) for t in (time_table, amp_table, width_table)]
    image = pl.pallas_call(
        functools.partial(migrate, signal.shape[0]),
        out_shape=jax.ShapeDtypeStruct((DEPTH, CELLS), jnp.float32),
        in_specs=[pl.BlockSpec(memory_space=pltpu.SMEM)]
        + [pl.BlockSpec(memory_space=pltpu.VMEM)] * 4,
        out_specs=pl.BlockSpec(memory_space=pltpu.VMEM),
        scratch_shapes=[pltpu.VMEM((2, CLASSES * ROWS, 128), jnp.float32)],
        name="migrate",
    )(meta, signal, *tables)
    planes = image.reshape(DEPTH, 1, CELLS)
    slab = lax.all_to_all(planes, "offs", split_axis=0, concat_axis=1, tiled=True)
    return slab[None]


def solution(mesh):
    return jax.shard_map(
        body,
        mesh=mesh,
        in_specs=(
            P("offs", "tile", None, None),
            P("offs", "tile"),
            P("offs", "tile", None),
            P("offs", "tile", None),
            P(None, "tile", None),
            P(None, "tile", None),
            P(None, "tile", None),
        ),
        out_specs=P("tile", "offs", None, None),
        check_vma=False,
    )
```

```python
import jax
import jax.numpy as jnp
from jax import lax
from jax.experimental import pallas as pl
from jax.experimental.pallas import tpu as pltpu
from jax.sharding import PartitionSpec as P

CELLS = 128
DEPTH = 16
ROWS = 16
LANES = 128
SPLIT = jnp.bfloat16
HALF_WIDTHS = (1, 2, 4)
CLASSES = len(HALF_WIDTHS)
EDGE = 16
REACH = 4
MESH = pl.DeviceIdType.MESH


def band():
    depth = LANES + EDGE
    k = lax.broadcasted_iota(jnp.int32, (depth, CLASSES * LANES), 0)
    column = lax.broadcasted_iota(jnp.int32, (depth, CLASSES * LANES), 1)
    far = jnp.where(k < LANES + 2 * REACH, k - LANES - 2 * REACH, 4 * LANES)
    place = jnp.where(k < LANES + REACH, k, far)
    apart = jnp.abs(place - (column & (LANES - 1)))
    top = jnp.where(column < LANES, HALF_WIDTHS[0] + 1, HALF_WIDTHS[1] + 1)
    top = jnp.where(column < 2 * LANES, top, HALF_WIDTHS[2] + 1)
    return jnp.maximum(top - apart, 0).astype(jnp.float32).astype(SPLIT)


def halves(x):
    high = x.astype(SPLIT)
    return high, (x - high.astype(jnp.float32)).astype(SPLIT)


def migrate(
    traces, src, rec, aper, time_hbm, amp_hbm, width_hbm, out,
    raw, own, send, recv, note, notes, notes_s, src_s, rec_s, aper_s,
    times, amps, widths, weights, filtered, image,
    local, send_sem, recv_sem, note_send, note_recv, row_send, row_recv,
):
    me = lax.axis_index("tile")
    column = lax.axis_index("offs")
    tiles = recv.shape[0]
    classes = out.shape[0]
    blocks, pair = own.shape[0], own.shape[1]
    samples = raw.shape[2]
    loads = [
        pltpu.make_async_copy(a, b, local.at[i])
        for i, (a, b) in enumerate(
            (
                (aper.at[0], aper_s),
                (src, src_s),
                (rec.at[0], rec_s),
                (traces.at[0], raw),
                (time_hbm, times),
                (amp_hbm, amps),
                (width_hbm, widths),
            )
        )
    ]
    barrier = pltpu.get_barrier_semaphore()
    for load in loads:
        load.start()

    def greet_tile(k, carry):
        pl.semaphore_signal(
            barrier, inc=1, device_id={"tile": lax.rem(me + k, tiles)}, device_id_type=MESH
        )
        return carry

    def greet_offs(k, carry):
        pl.semaphore_signal(
            barrier, inc=1, device_id={"offs": lax.rem(column + k, classes)}, device_id_type=MESH
        )
        return carry

    lax.fori_loop(1, tiles, greet_tile, 0)
    lax.fori_loop(1, classes, greet_offs, 0)

    weights[...] = band()
    image[...] = jnp.zeros_like(image)
    own[:, :, pl.ds(ROWS - 8, 8), :] = jnp.zeros((blocks, pair, 8, LANES), jnp.float32)
    for load in loads[:4]:
        load.wait()

    def lay(b, carry):
        for c in range(samples // LANES):
            own[b, :, c, :] = raw[b, :, pl.ds(c * LANES, LANES)]
        rest = samples % LANES
        if rest:
            own[b, :, samples // LANES, pl.ds(0, rest)] = raw[b, :, pl.ds(samples - rest, rest)]
        return carry

    lax.fori_loop(0, blocks, lay, 0)
    lane = lax.broadcasted_iota(jnp.int32, (1, LANES), 1)

    def pack(k, carry):
        peer = lax.rem(me + k, tiles)
        first, second, named = jnp.int32(0), jnp.int32(0), jnp.int32(0)
        for b in range(blocks):
            hit = (aper_s[0, b] == peer) | (aper_s[1, b] == peer)
            first = jnp.where(hit & (named == 0), b, first)
            second = jnp.where(hit & (named == 1), b, second)
            named = named + hit.astype(jnp.int32)
        line = jnp.zeros((1, LANES), jnp.int32)
        for s, b in enumerate((first, second)):
            send[k, s] = own[b]
            line = jnp.where(lane == 4 * s, (named > s).astype(jnp.int32), line)
            line = jnp.where(lane == 4 * s + 1, src_s[0, b], line)
            line = jnp.where(lane == 4 * s + 2, rec_s[0, b], line)
            line = jnp.where(lane == 4 * s + 3, rec_s[1, b], line)
        note[pl.ds(k, 1)] = line
        return carry

    lax.fori_loop(0, tiles, pack, 0)
    notes[pl.ds(0, 1)] = note[pl.ds(0, 1)]
    recv[0] = send[0]

    def note_copy(k):
        return pltpu.make_async_remote_copy(
            note.at[pl.ds(k, 1)], notes.at[pl.ds(k, 1)], note_send.at[k], note_recv.at[k],
            device_id={"tile": lax.rem(me + k, tiles)}, device_id_type=MESH,
        )

    def trace_copy(k):
        return pltpu.make_async_remote_copy(
            send.at[k], recv.at[k], send_sem.at[k], recv_sem.at[k],
            device_id={"tile": lax.rem(me + k, tiles)}, device_id_type=MESH,
        )

    def each(first, last, action):
        def step(k, carry):
            action(k)
            return carry

        lax.fori_loop(first, last, step, 0)

    pl.semaphore_wait(barrier, tiles + classes - 2)
    each(1, tiles, lambda k: note_copy(k).start())
    each(1, tiles, lambda k: trace_copy(k).start())
    for load in loads[4:]:
        load.wait()
    each(1, tiles, lambda k: note_copy(k).wait_recv())
    to_scalar = pltpu.make_async_copy(notes, notes_s, local.at[len(loads)])
    to_scalar.start()
    to_scalar.wait()
    wide = lax.broadcasted_iota(jnp.int32, (ROWS, LANES), 1)

    def source(k):
        parts = []
        for s in range(2):
            for i in range(pair):
                x = recv[k, s, i]
                edge = jnp.where(
                    wide < REACH,
                    pltpu.roll(x, ROWS - 1, 0),
                    pltpu.roll(pltpu.roll(x, 1, 0), 2 * REACH, 1),
                )[:, :EDGE]
                xs, es = halves(x), halves(edge)
                parts += [jnp.concatenate([a, b], 1) for a, b in zip(xs, es)]
        total = jnp.dot(
            jnp.concatenate(parts, 0), weights[...], preferred_element_type=jnp.float32
        )
        for n in range(2 * pair):
            for c, h in enumerate(HALF_WIDTHS):
                lanes = slice(c * LANES, (c + 1) * LANES)
                high = total[2 * n * ROWS : (2 * n + 1) * ROWS, lanes]
                low = total[(2 * n + 1) * ROWS : (2 * n + 2) * ROWS, lanes]
                filtered[n, pl.ds(c * ROWS, ROWS)] = (high + low) * (1.0 / (h + 1) ** 2)
        sums = [jnp.zeros((8, LANES), jnp.float32) for _ in range(DEPTH // 8)]
        for s in range(2):
            live = notes_s[k, 4 * s] > 0
            node = notes_s[k, 4 * s + 1]
            source_time, source_amp, source_width = times[node], amps[node], widths[node]
            for i in range(pair):
                node = notes_s[k, 4 * s + 2 + i]
                sample = source_time + times[node]
                weight = jnp.where(live, source_amp * amps[node], 0.0)
                row = jnp.maximum(source_width, widths[node]) * ROWS + (sample >> 7)
                place = sample & (LANES - 1)
                for z in range(DEPTH // 8):
                    cut = slice(8 * z, 8 * z + 8)
                    picked = jnp.zeros((8, LANES), jnp.float32)
                    for r in range(CLASSES * ROWS):
                        values = jnp.broadcast_to(filtered[2 * s + i, pl.ds(r, 1)], (8, LANES))
                        values = jnp.take_along_axis(
                            values, place[cut], axis=1, mode="promise_in_bounds"
                        )
                        picked = jnp.where(row[cut] == r, values, picked)
                    sums[z] += weight[cut] * picked
        image[...] += jnp.concatenate(sums, 0)

    source(jnp.int32(0))

    def arrive(k, carry):
        trace_copy(k).wait_recv()
        source(k)
        return carry

    lax.fori_loop(1, tiles, arrive, 0)

    def row_copy(k):
        to = lax.rem(column + k, classes)
        return pltpu.make_async_remote_copy(
            image.at[pl.ds(to, 1)], out.at[pl.ds(column, 1)], row_send.at[k], row_recv.at[k],
            device_id={"offs": to}, device_id_type=MESH,
        )

    each(1, classes, lambda k: row_copy(k).start())
    out[pl.ds(column, 1)] = image[pl.ds(column, 1)]
    each(1, tiles, lambda k: note_copy(k).wait_send())
    each(1, tiles, lambda k: trace_copy(k).wait_send())
    each(1, classes, lambda k: row_copy(k).wait_send())
    each(1, classes, lambda k: row_copy(k).wait_recv())


def body(traces, src_node, rec_node, aperture, time_table, amp_table, width_table):
    tiles = lax.axis_size("tile")
    classes = lax.axis_size("offs")
    _, blocks, pair, samples = traces.shape
    nodes = time_table.shape[0]
    tables = [t.reshape(nodes, DEPTH, CELLS) for t in (time_table, amp_table, width_table)]
    f32, i32 = jnp.float32, jnp.int32
    dma = pltpu.SemaphoreType.DMA
    slab = pl.pallas_call(
        migrate,
        out_shape=jax.ShapeDtypeStruct((classes, CELLS), f32),
        in_specs=[pl.BlockSpec(memory_space=pl.ANY)] * 7,
        out_specs=pl.BlockSpec(memory_space=pltpu.VMEM),
        scratch_shapes=[
            pltpu.VMEM((blocks, pair, samples), f32),
            pltpu.VMEM((blocks, pair, ROWS, LANES), f32),
            pltpu.VMEM((tiles, 2, pair, ROWS, LANES), f32),
            pltpu.VMEM((tiles, 2, pair, ROWS, LANES), f32),
            pltpu.VMEM((tiles, LANES), i32),
            pltpu.VMEM((tiles, LANES), i32),
            pltpu.SMEM((tiles, LANES), i32),
            pltpu.SMEM((1, blocks), i32),
            pltpu.SMEM((pair, blocks), i32),
            pltpu.SMEM((2, blocks), i32),
            pltpu.VMEM((nodes, DEPTH, CELLS), i32),
            pltpu.VMEM((nodes, DEPTH, CELLS), f32),
            pltpu.VMEM((nodes, DEPTH, CELLS), i32),
            pltpu.VMEM((LANES + EDGE, CLASSES * LANES), SPLIT),
            pltpu.VMEM((2 * pair, CLASSES * ROWS, LANES), f32),
            pltpu.VMEM((DEPTH, CELLS), f32),
            dma((8,)),
            dma((tiles,)),
            dma((tiles,)),
            dma((tiles,)),
            dma((tiles,)),
            dma((classes,)),
            dma((classes,)),
        ],
        compiler_params=pltpu.CompilerParams(collective_id=0, has_side_effects=True),
        name="migrate",
    )(traces, src_node, jnp.swapaxes(rec_node, 1, 2), jnp.swapaxes(aperture, 1, 2), *tables)
    return slab[None, None]


def solution(mesh):
    return jax.shard_map(
        body,
        mesh=mesh,
        in_specs=(
            P("offs", "tile", None, None),
            P("offs", "tile"),
            P("offs", "tile", None),
            P("offs", "tile", None),
            P(None, "tile", None),
            P(None, "tile", None),
            P(None, "tile", None),
        ),
        out_specs=P("tile", "offs", None, None),
        check_vma=False,
    )
```

```python
import jax
import jax.numpy as jnp
from jax import lax
from jax.experimental import pallas as pl
from jax.experimental.pallas import tpu as pltpu
from jax.sharding import PartitionSpec as P

CELLS = 128
DEPTH = 16
ROWS = 16
LANES = 128
SPLIT = jnp.bfloat16
HALF_WIDTHS = (1, 2, 4)
CLASSES = len(HALF_WIDTHS)
EDGE = 16
REACH = 4
MESH = pl.DeviceIdType.MESH
ORDER = (1, 2, 14, 8, 4, 12, 15, 3, 13, 6, 10, 7, 5, 11, 9)


def band():
    depth = LANES + EDGE
    k = lax.broadcasted_iota(jnp.int32, (depth, CLASSES * LANES), 0)
    column = lax.broadcasted_iota(jnp.int32, (depth, CLASSES * LANES), 1)
    far = jnp.where(k < LANES + 2 * REACH, k - LANES - 2 * REACH, 4 * LANES)
    place = jnp.where(k < LANES + REACH, k, far)
    apart = jnp.abs(place - (column & (LANES - 1)))
    top = jnp.where(column < LANES, HALF_WIDTHS[0] + 1, HALF_WIDTHS[1] + 1)
    top = jnp.where(column < 2 * LANES, top, HALF_WIDTHS[2] + 1)
    return jnp.maximum(top - apart, 0).astype(jnp.float32).astype(SPLIT)


def halves(x):
    high = x.astype(SPLIT)
    return high, (x - high.astype(jnp.float32)).astype(SPLIT)


def migrate(
    traces, src, rec, aper, time_hbm, amp_hbm, width_hbm, out,
    raw, own, send, recv, note, notes, notes_s, src_s, rec_s, aper_s,
    times, amps, widths, weights, filtered, image,
    local, send_sem, recv_sem, note_send, note_recv, row_send, row_recv,
):
    me = lax.axis_index("tile")
    column = lax.axis_index("offs")
    tiles = recv.shape[0]
    classes = out.shape[0]
    blocks, pair = own.shape[0], own.shape[1]
    samples = raw.shape[2]
    loads = [
        pltpu.make_async_copy(a, b, local.at[i])
        for i, (a, b) in enumerate(
            (
                (aper.at[0], aper_s),
                (src, src_s),
                (rec.at[0], rec_s),
                (traces.at[0], raw),
                (time_hbm, times),
                (amp_hbm, amps),
                (width_hbm, widths),
            )
        )
    ]
    barrier = pltpu.get_barrier_semaphore()
    for load in loads:
        load.start()

    def greet_tile(k, carry):
        pl.semaphore_signal(
            barrier, inc=1, device_id={"tile": lax.rem(me + k, tiles)}, device_id_type=MESH
        )
        return carry

    def greet_offs(k, carry):
        pl.semaphore_signal(
            barrier, inc=1, device_id={"offs": lax.rem(column + k, classes)}, device_id_type=MESH
        )
        return carry

    lax.fori_loop(1, tiles, greet_tile, 0)
    lax.fori_loop(1, classes, greet_offs, 0)

    weights[...] = band()
    image[...] = jnp.zeros_like(image)
    own[:, :, pl.ds(ROWS - 8, 8), :] = jnp.zeros((blocks, pair, 8, LANES), jnp.float32)
    for load in loads[:4]:
        load.wait()

    def lay(b, carry):
        for c in range(samples // LANES):
            own[b, :, c, :] = raw[b, :, pl.ds(c * LANES, LANES)]
        rest = samples % LANES
        if rest:
            own[b, :, samples // LANES, pl.ds(0, rest)] = raw[b, :, pl.ds(samples - rest, rest)]
        return carry

    lax.fori_loop(0, blocks, lay, 0)
    lane = lax.broadcasted_iota(jnp.int32, (1, LANES), 1)

    def pack(k, carry):
        peer = lax.rem(me + k, tiles)
        first, second, named = jnp.int32(0), jnp.int32(0), jnp.int32(0)
        for b in range(blocks):
            hit = (aper_s[0, b] == peer) | (aper_s[1, b] == peer)
            first = jnp.where(hit & (named == 0), b, first)
            second = jnp.where(hit & (named == 1), b, second)
            named = named + hit.astype(jnp.int32)
        line = jnp.zeros((1, LANES), jnp.int32)
        for s, b in enumerate((first, second)):
            send[k, s] = own[b]
            line = jnp.where(lane == 4 * s, (named > s).astype(jnp.int32), line)
            line = jnp.where(lane == 4 * s + 1, src_s[0, b], line)
            line = jnp.where(lane == 4 * s + 2, rec_s[0, b], line)
            line = jnp.where(lane == 4 * s + 3, rec_s[1, b], line)
        note[pl.ds(k, 1)] = line
        return carry

    lax.fori_loop(0, tiles, pack, 0)
    notes[pl.ds(0, 1)] = note[pl.ds(0, 1)]
    recv[0] = send[0]

    def note_copy(k):
        return pltpu.make_async_remote_copy(
            note.at[pl.ds(k, 1)], notes.at[pl.ds(k, 1)], note_send.at[k], note_recv.at[k],
            device_id={"tile": lax.rem(me + k, tiles)}, device_id_type=MESH,
        )

    def trace_copy(k):
        return pltpu.make_async_remote_copy(
            send.at[k], recv.at[k], send_sem.at[k], recv_sem.at[k],
            device_id={"tile": lax.rem(me + k, tiles)}, device_id_type=MESH,
        )

    def each(first, last, action):
        def step(k, carry):
            action(k)
            return carry

        lax.fori_loop(first, last, step, 0)

    def turn(j):
        k = jnp.int32(0)
        for place, offset in enumerate(ORDER, 1):
            k = jnp.where(j == place, offset, k)
        return k

    pl.semaphore_wait(barrier, tiles + classes - 2)
    each(1, tiles, lambda k: note_copy(k).start())
    each(1, tiles, lambda j: trace_copy(turn(j)).start())
    for load in loads[4:]:
        load.wait()
    each(1, tiles, lambda k: note_copy(k).wait_recv())
    to_scalar = pltpu.make_async_copy(notes, notes_s, local.at[len(loads)])
    to_scalar.start()
    to_scalar.wait()
    wide = lax.broadcasted_iota(jnp.int32, (ROWS, LANES), 1)

    def source(k):
        parts = []
        for s in range(2):
            for i in range(pair):
                x = recv[k, s, i]
                edge = jnp.where(
                    wide < REACH,
                    pltpu.roll(x, ROWS - 1, 0),
                    pltpu.roll(pltpu.roll(x, 1, 0), 2 * REACH, 1),
                )[:, :EDGE]
                xs, es = halves(x), halves(edge)
                parts += [jnp.concatenate([a, b], 1) for a, b in zip(xs, es)]
        total = jnp.dot(
            jnp.concatenate(parts, 0), weights[...], preferred_element_type=jnp.float32
        )
        for n in range(2 * pair):
            for c, h in enumerate(HALF_WIDTHS):
                lanes = slice(c * LANES, (c + 1) * LANES)
                high = total[2 * n * ROWS : (2 * n + 1) * ROWS, lanes]
                low = total[(2 * n + 1) * ROWS : (2 * n + 2) * ROWS, lanes]
                filtered[n, pl.ds(c * ROWS, ROWS)] = (high + low) * (1.0 / (h + 1) ** 2)
        sums = [jnp.zeros((8, LANES), jnp.float32) for _ in range(DEPTH // 8)]
        for s in range(2):
            live = notes_s[k, 4 * s] > 0
            node = notes_s[k, 4 * s + 1]
            source_time, source_amp, source_width = times[node], amps[node], widths[node]
            for i in range(pair):
                node = notes_s[k, 4 * s + 2 + i]
                sample = source_time + times[node]
                weight = jnp.where(live, source_amp * amps[node], 0.0)
                row = jnp.maximum(source_width, widths[node]) * ROWS + (sample >> 7)
                place = sample & (LANES - 1)
                for z in range(DEPTH // 8):
                    cut = slice(8 * z, 8 * z + 8)
                    picked = jnp.zeros((8, LANES), jnp.float32)
                    for r in range(CLASSES * ROWS):
                        values = jnp.broadcast_to(filtered[2 * s + i, pl.ds(r, 1)], (8, LANES))
                        values = jnp.take_along_axis(
                            values, place[cut], axis=1, mode="promise_in_bounds"
                        )
                        picked = jnp.where(row[cut] == r, values, picked)
                    sums[z] += weight[cut] * picked
        image[...] += jnp.concatenate(sums, 0)

    source(jnp.int32(0))

    def arrive(j, carry):
        k = turn(j)
        trace_copy(k).wait_recv()
        source(k)
        return carry

    lax.fori_loop(1, tiles, arrive, 0)

    def row_copy(k):
        to = lax.rem(column + k, classes)
        return pltpu.make_async_remote_copy(
            image.at[pl.ds(to, 1)], out.at[pl.ds(column, 1)], row_send.at[k], row_recv.at[k],
            device_id={"offs": to}, device_id_type=MESH,
        )

    each(1, classes, lambda k: row_copy(k).start())
    out[pl.ds(column, 1)] = image[pl.ds(column, 1)]
    each(1, tiles, lambda k: note_copy(k).wait_send())
    each(1, tiles, lambda k: trace_copy(k).wait_send())
    each(1, classes, lambda k: row_copy(k).wait_send())
    each(1, classes, lambda k: row_copy(k).wait_recv())


def body(traces, src_node, rec_node, aperture, time_table, amp_table, width_table):
    tiles = lax.axis_size("tile")
    classes = lax.axis_size("offs")
    _, blocks, pair, samples = traces.shape
    nodes = time_table.shape[0]
    tables = [t.reshape(nodes, DEPTH, CELLS) for t in (time_table, amp_table, width_table)]
    f32, i32 = jnp.float32, jnp.int32
    dma = pltpu.SemaphoreType.DMA
    slab = pl.pallas_call(
        migrate,
        out_shape=jax.ShapeDtypeStruct((classes, CELLS), f32),
        in_specs=[pl.BlockSpec(memory_space=pl.ANY)] * 7,
        out_specs=pl.BlockSpec(memory_space=pltpu.VMEM),
        scratch_shapes=[
            pltpu.VMEM((blocks, pair, samples), f32),
            pltpu.VMEM((blocks, pair, ROWS, LANES), f32),
            pltpu.VMEM((tiles, 2, pair, ROWS, LANES), f32),
            pltpu.VMEM((tiles, 2, pair, ROWS, LANES), f32),
            pltpu.VMEM((tiles, LANES), i32),
            pltpu.VMEM((tiles, LANES), i32),
            pltpu.SMEM((tiles, LANES), i32),
            pltpu.SMEM((1, blocks), i32),
            pltpu.SMEM((pair, blocks), i32),
            pltpu.SMEM((2, blocks), i32),
            pltpu.VMEM((nodes, DEPTH, CELLS), i32),
            pltpu.VMEM((nodes, DEPTH, CELLS), f32),
            pltpu.VMEM((nodes, DEPTH, CELLS), i32),
            pltpu.VMEM((LANES + EDGE, CLASSES * LANES), SPLIT),
            pltpu.VMEM((2 * pair, CLASSES * ROWS, LANES), f32),
            pltpu.VMEM((DEPTH, CELLS), f32),
            dma((8,)),
            dma((tiles,)),
            dma((tiles,)),
            dma((tiles,)),
            dma((tiles,)),
            dma((classes,)),
            dma((classes,)),
        ],
        compiler_params=pltpu.CompilerParams(collective_id=0, has_side_effects=True),
        name="migrate",
    )(traces, src_node, jnp.swapaxes(rec_node, 1, 2), jnp.swapaxes(aperture, 1, 2), *tables)
    return slab[None, None]


def solution(mesh):
    return jax.shard_map(
        body,
        mesh=mesh,
        in_specs=(
            P("offs", "tile", None, None),
            P("offs", "tile"),
            P("offs", "tile", None),
            P("offs", "tile", None),
            P(None, "tile", None),
            P(None, "tile", None),
            P(None, "tile", None),
        ),
        out_specs=P("tile", "offs", None, None),
        check_vma=False,
    )
```

```python
import jax
import jax.numpy as jnp
from jax import lax
from jax.experimental import pallas as pl
from jax.experimental.pallas import tpu as pltpu
from jax.sharding import PartitionSpec as P

CELLS = 128
DEPTH = 16
ROWS = 16
LANES = 128
SPLIT = jnp.bfloat16
HALF_WIDTHS = (1, 2, 4)
CLASSES = len(HALF_WIDTHS)
EDGE = 16
REACH = 4
GATHERED = 1
MESH = pl.DeviceIdType.MESH
ORDER = (1, 2, 14, 8, 4, 12, 15, 3, 13, 6, 10, 7, 5, 11, 9)


def band():
    depth = LANES + EDGE
    k = lax.broadcasted_iota(jnp.int32, (depth, CLASSES * LANES), 0)
    column = lax.broadcasted_iota(jnp.int32, (depth, CLASSES * LANES), 1)
    far = jnp.where(k < LANES + 2 * REACH, k - LANES - 2 * REACH, 4 * LANES)
    place = jnp.where(k < LANES + REACH, k, far)
    apart = jnp.abs(place - (column & (LANES - 1)))
    top = jnp.where(column < LANES, HALF_WIDTHS[0] + 1, HALF_WIDTHS[1] + 1)
    top = jnp.where(column < 2 * LANES, top, HALF_WIDTHS[2] + 1)
    return jnp.maximum(top - apart, 0).astype(jnp.float32).astype(SPLIT)


def halves(x):
    high = x.astype(SPLIT)
    return high, (x - high.astype(jnp.float32)).astype(SPLIT)


def migrate(
    traces, src, rec, aper, time_hbm, amp_hbm, width_hbm, out,
    raw, own, send, recv, note, notes, notes_s, src_s, rec_s, aper_s,
    times, amps, widths, weights, filtered, image, spread, lines, rows,
    local, send_sem, recv_sem, note_send, note_recv, row_send, row_recv,
):
    me = lax.axis_index("tile")
    column = lax.axis_index("offs")
    tiles = recv.shape[0]
    classes = out.shape[0]
    blocks, pair = own.shape[0], own.shape[1]
    samples = raw.shape[2]
    loads = [
        pltpu.make_async_copy(a, b, local.at[i])
        for i, (a, b) in enumerate(
            (
                (aper.at[0], aper_s),
                (src, src_s),
                (rec.at[0], rec_s),
                (traces.at[0], raw),
                (time_hbm, times),
                (amp_hbm, amps),
                (width_hbm, widths),
            )
        )
    ]
    barrier = pltpu.get_barrier_semaphore()
    for k in range(1, tiles):
        pl.semaphore_signal(
            barrier, inc=1, device_id={"tile": lax.rem(me + k, tiles)}, device_id_type=MESH
        )
    for load in loads:
        load.start()
    for k in range(1, classes):
        pl.semaphore_signal(
            barrier, inc=1, device_id={"offs": lax.rem(column + k, classes)}, device_id_type=MESH
        )

    weights[...] = band()
    image[...] = jnp.zeros_like(image)
    spread[...] = jnp.zeros_like(spread)
    own[:, :, pl.ds(ROWS - 8, 8), :] = jnp.zeros((blocks, pair, 8, LANES), jnp.float32)
    for load in loads[:4]:
        load.wait()

    def lay(b, carry):
        for c in range(samples // LANES):
            own[b, :, c, :] = raw[b, :, pl.ds(c * LANES, LANES)]
        rest = samples % LANES
        if rest:
            own[b, :, samples // LANES, pl.ds(0, rest)] = raw[b, :, pl.ds(samples - rest, rest)]
        return carry

    lax.fori_loop(0, blocks, lay, 0)
    lane = lax.broadcasted_iota(jnp.int32, (1, LANES), 1)

    def pack(k, carry):
        peer = lax.rem(me + k, tiles)
        first, second, named = jnp.int32(0), jnp.int32(0), jnp.int32(0)
        for b in range(blocks):
            hit = (aper_s[0, b] == peer) | (aper_s[1, b] == peer)
            first = jnp.where(hit & (named == 0), b, first)
            second = jnp.where(hit & (named == 1), b, second)
            named = named + hit.astype(jnp.int32)
        line = jnp.zeros((1, LANES), jnp.int32)
        for s, b in enumerate((first, second)):
            send[k, s] = own[b]
            line = jnp.where(lane == 4 * s, (named > s).astype(jnp.int32), line)
            line = jnp.where(lane == 4 * s + 1, src_s[0, b], line)
            line = jnp.where(lane == 4 * s + 2, rec_s[0, b], line)
            line = jnp.where(lane == 4 * s + 3, rec_s[1, b], line)
        note[pl.ds(k, 1)] = line
        return carry

    lax.fori_loop(0, tiles, pack, 0)
    notes[pl.ds(0, 1)] = note[pl.ds(0, 1)]
    recv[0] = send[0]

    def note_copy(k):
        return pltpu.make_async_remote_copy(
            note.at[pl.ds(k, 1)], notes.at[pl.ds(k, 1)], note_send, note_recv,
            device_id={"tile": lax.rem(me + k, tiles)}, device_id_type=MESH,
        )

    def trace_copy(k):
        return pltpu.make_async_remote_copy(
            send.at[k], recv.at[k], send_sem.at[k], recv_sem.at[k],
            device_id={"tile": lax.rem(me + k, tiles)}, device_id_type=MESH,
        )

    def each(first, last, action):
        def step(k, carry):
            action(k)
            return carry

        lax.fori_loop(first, last, step, 0)

    def turn(j):
        k = jnp.int32(0)
        for place, offset in enumerate(ORDER, 1):
            k = jnp.where(j == place, offset, k)
        return k

    pl.semaphore_wait(barrier, tiles + classes - 2)
    each(1, tiles, lambda k: note_copy(k).start())
    each(1, tiles, lambda j: trace_copy(turn(j)).start())
    for load in loads[4:]:
        load.wait()
    others = pl.ds(0, tiles - 1)
    pltpu.make_async_copy(notes.at[others], notes.at[others], note_recv).wait()
    to_scalar = pltpu.make_async_copy(notes, notes_s, local.at[len(loads)])
    to_scalar.start()
    to_scalar.wait()
    pltpu.make_async_copy(note.at[others], note.at[others], note_send).wait()
    wide = lax.broadcasted_iota(jnp.int32, (ROWS, LANES), 1)
    deep = lax.broadcasted_iota(jnp.int32, (ROWS, LANES), 0)
    eight = lax.broadcasted_iota(jnp.int32, (8, LANES), 0)
    ends = jnp.where(deep < 2 * REACH, deep - 2 * REACH, 4 * LANES)
    ends = jnp.where(deep < REACH, deep + LANES, ends)
    spots = [deep + ROWS * n for n in range(LANES // ROWS)] + [ends]
    spots = [x.astype(jnp.float32).astype(SPLIT) for x in spots]
    none = jnp.zeros((ROWS, LANES), SPLIT)

    def source(k):
        parts = []
        for s in range(2):
            for i in range(pair):
                x = recv[k, s, i]
                edge = jnp.where(
                    wide < REACH,
                    pltpu.roll(x, ROWS - 1, 0),
                    pltpu.roll(pltpu.roll(x, 1, 0), 2 * REACH, 1),
                )[:, :EDGE]
                xs, es = halves(x), halves(edge)
                parts += [jnp.concatenate([a, b], 1) for a, b in zip(xs, es)]
        total = jnp.dot(
            jnp.concatenate(parts[: 2 * GATHERED], 0),
            weights[...],
            preferred_element_type=jnp.float32,
        )
        for n in range(GATHERED):
            for c, h in enumerate(HALF_WIDTHS):
                lanes = slice(c * LANES, (c + 1) * LANES)
                high = total[2 * n * ROWS : (2 * n + 1) * ROWS, lanes]
                low = total[(2 * n + 1) * ROWS : (2 * n + 2) * ROWS, lanes]
                filtered[n, pl.ds(c * ROWS, ROWS)] = (high + low) * (1.0 / (h + 1) ** 2)
        sums = [jnp.zeros((8, LANES), jnp.float32) for _ in range(DEPTH // 8)]
        jobs = []
        for s in range(2):
            live = notes_s[k, 4 * s] > 0
            node = notes_s[k, 4 * s + 1]
            source_time, source_amp, source_width = times[node], amps[node], widths[node]
            for i in range(pair):
                node = notes_s[k, 4 * s + 2 + i]
                sample = source_time + times[node]
                weight = jnp.where(live, source_amp * amps[node], 0.0)
                jobs.append((sample, weight, jnp.maximum(source_width, widths[node])))

        def gather(n, z):
            sample, weight, width = jobs[n]
            row = width * ROWS + (sample >> 7)
            place = sample & (LANES - 1)
            cut = slice(8 * z, 8 * z + 8)
            picked = jnp.zeros((8, LANES), jnp.float32)
            for r in range(CLASSES * ROWS):
                values = jnp.broadcast_to(filtered[n, pl.ds(r, 1)], (8, LANES))
                values = jnp.take_along_axis(
                    values, place[cut], axis=1, mode="promise_in_bounds"
                )
                picked = jnp.where(row[cut] == r, values, picked)
            sums[z] += weight[cut] * picked

        def prepare(n):
            sample, weight, width = jobs[n]
            tops = [h + 1 for h in HALF_WIDTHS]
            top = jnp.where(width == 0, tops[0], jnp.where(width == 1, tops[1], tops[2]))
            scale = jnp.where(
                width == 0,
                1.0 / tops[0] ** 2,
                jnp.where(width == 1, 1.0 / tops[1] ** 2, 1.0 / tops[2] ** 2),
            )
            m = n - GATHERED
            lines[m, 0] = (sample & (LANES - 1)).astype(jnp.float32)
            lines[m, 1] = top.astype(jnp.float32)
            lines[m, 2] = weight * scale
            rows[m] = sample >> 7

        def product(n, zs):
            m = n - GATHERED
            cols = []
            for z in zs:
                at = jnp.broadcast_to(lines[m, 0, pl.ds(z, 1)], (ROWS, LANES)).astype(SPLIT)
                top = jnp.broadcast_to(lines[m, 1, pl.ds(z, 1)], (ROWS, LANES)).astype(SPLIT)
                cols.append(
                    jnp.concatenate([jnp.maximum(top - jnp.abs(x - at), none) for x in spots], 0)
                )
            got = jnp.dot(
                jnp.concatenate(parts[2 * n : 2 * n + 2], 0),
                jnp.concatenate(cols, 1),
                preferred_element_type=jnp.float32,
            )
            got = got[:ROWS] + got[ROWS:]
            for q, z in enumerate(zs):
                lanes = slice(q * LANES, (q + 1) * LANES)
                row = jnp.broadcast_to(rows[m, pl.ds(z, 1)], (8, LANES)) - eight
                picked = jnp.where(row == 0, got[:8, lanes], 0.0)
                picked = jnp.where(row == 8, got[8:, lanes], picked)
                spread[z] += picked * jnp.broadcast_to(lines[m, 2, pl.ds(z, 1)], (8, LANES))

        products = [(n, (z, z + 1)) for n in range(GATHERED, 2 * pair) for z in range(0, DEPTH, 2)]
        gathers = [(n, z) for n in range(GATHERED) for z in range(DEPTH // 8)]
        for n in range(GATHERED, 2 * pair):
            prepare(n)
        total_steps = max(len(products), len(gathers))
        for step in range(total_steps):
            for g in range(step * len(gathers) // total_steps, (step + 1) * len(gathers) // total_steps):
                gather(*gathers[g])
            for p in range(step * len(products) // total_steps, (step + 1) * len(products) // total_steps):
                product(*products[p])
        image[...] += jnp.concatenate(sums, 0)

    source(jnp.int32(0))

    def arrive(j, carry):
        k = turn(j)
        trace_copy(k).wait_recv()
        source(k)
        trace_copy(k).wait_send()
        return carry

    lax.fori_loop(1, tiles, arrive, 0)
    image[...] += jnp.sum(spread[...], axis=1)

    def row_copy(k):
        to = lax.rem(column + k, classes)
        return pltpu.make_async_remote_copy(
            image.at[pl.ds(to, 1)], out.at[pl.ds(column, 1)], row_send, row_recv,
            device_id={"offs": to}, device_id_type=MESH,
        )

    each(1, classes, lambda k: row_copy(k).start())
    mine = pltpu.make_async_copy(
        image.at[pl.ds(column, 1)], out.at[pl.ds(column, 1)], local.at[len(loads)]
    )
    mine.start()
    mine.wait()
    rest = pl.ds(0, classes - 1)
    pltpu.make_async_copy(image.at[rest], image.at[rest], row_send).wait()
    pltpu.make_async_copy(image.at[rest], image.at[rest], row_recv).wait()


def body(traces, src_node, rec_node, aperture, time_table, amp_table, width_table):
    tiles = lax.axis_size("tile")
    classes = lax.axis_size("offs")
    _, blocks, pair, samples = traces.shape
    nodes = time_table.shape[0]
    tables = [t.reshape(nodes, DEPTH, CELLS) for t in (time_table, amp_table, width_table)]
    f32, i32 = jnp.float32, jnp.int32
    dma = pltpu.SemaphoreType.DMA
    slab = pl.pallas_call(
        migrate,
        out_shape=jax.ShapeDtypeStruct((classes, CELLS), f32),
        in_specs=[pl.BlockSpec(memory_space=pl.ANY)] * 7,
        out_specs=pl.BlockSpec(memory_space=pl.ANY),
        scratch_shapes=[
            pltpu.VMEM((blocks, pair, samples), f32),
            pltpu.VMEM((blocks, pair, ROWS, LANES), f32),
            pltpu.VMEM((tiles, 2, pair, ROWS, LANES), f32),
            pltpu.VMEM((tiles, 2, pair, ROWS, LANES), f32),
            pltpu.VMEM((tiles, LANES), i32),
            pltpu.VMEM((tiles, LANES), i32),
            pltpu.SMEM((tiles, LANES), i32),
            pltpu.SMEM((1, blocks), i32),
            pltpu.SMEM((pair, blocks), i32),
            pltpu.SMEM((2, blocks), i32),
            pltpu.VMEM((nodes, DEPTH, CELLS), i32),
            pltpu.VMEM((nodes, DEPTH, CELLS), f32),
            pltpu.VMEM((nodes, DEPTH, CELLS), i32),
            pltpu.VMEM((LANES + EDGE, CLASSES * LANES), SPLIT),
            pltpu.VMEM((2 * pair, CLASSES * ROWS, LANES), f32),
            pltpu.VMEM((DEPTH, CELLS), f32),
            pltpu.VMEM((DEPTH, 8, CELLS), f32),
            pltpu.VMEM((4, 3, DEPTH, CELLS), f32),
            pltpu.VMEM((4, DEPTH, CELLS), i32),
            dma((8,)),
            dma((tiles,)),
            dma((tiles,)),
            dma,
            dma,
            dma,
            dma,
        ],
        compiler_params=pltpu.CompilerParams(collective_id=0, has_side_effects=True),
        name="migrate",
    )(traces, src_node, jnp.swapaxes(rec_node, 1, 2), jnp.swapaxes(aperture, 1, 2), *tables)
    return slab[None, None]


def solution(mesh):
    return jax.shard_map(
        body,
        mesh=mesh,
        in_specs=(
            P("offs", "tile", None, None),
            P("offs", "tile"),
            P("offs", "tile", None),
            P("offs", "tile", None),
            P(None, "tile", None),
            P(None, "tile", None),
            P(None, "tile", None),
        ),
        out_specs=P("tile", "offs", None, None),
        check_vma=False,
    )
```

```python
import jax
import jax.numpy as jnp
from jax import lax
from jax.experimental import pallas as pl
from jax.experimental.pallas import tpu as pltpu
from jax.sharding import PartitionSpec as P

CELLS = 128
DEPTH = 16
ROWS = 16
LANES = 128
SPLIT = jnp.bfloat16
HALF_WIDTHS = (1, 2, 4)
CLASSES = len(HALF_WIDTHS)
EDGE = 16
REACH = 4
GATHERED = 1
MESH = pl.DeviceIdType.MESH
ORDER = (1, 2, 14, 8, 4, 12, 15, 3, 13, 6, 10, 7, 5, 11, 9)


def band():
    depth = LANES + EDGE
    k = lax.broadcasted_iota(jnp.int32, (depth, CLASSES * LANES), 0)
    column = lax.broadcasted_iota(jnp.int32, (depth, CLASSES * LANES), 1)
    far = jnp.where(k < LANES + 2 * REACH, k - LANES - 2 * REACH, 4 * LANES)
    place = jnp.where(k < LANES + REACH, k, far)
    apart = jnp.abs(place - (column & (LANES - 1)))
    top = jnp.where(column < LANES, HALF_WIDTHS[0] + 1, HALF_WIDTHS[1] + 1)
    top = jnp.where(column < 2 * LANES, top, HALF_WIDTHS[2] + 1)
    return jnp.maximum(top - apart, 0).astype(jnp.float32).astype(SPLIT)


def halves(x):
    high = x.astype(SPLIT)
    return high, (x - high.astype(jnp.float32)).astype(SPLIT)


def migrate(
    traces, src, rec, aper, time_hbm, amp_hbm, width_hbm, out,
    raw, own, send, recv, note, notes, notes_s, src_s, rec_s, aper_s,
    times, amps, widths, weights, filtered, image, spread, lines, rows,
    local, send_sem, recv_sem, note_send, note_recv, row_send, row_recv,
):
    me = lax.axis_index("tile")
    column = lax.axis_index("offs")
    tiles = recv.shape[0]
    classes = out.shape[0]
    blocks, pair = own.shape[0], own.shape[1]
    samples = raw.shape[2]
    loads = [
        pltpu.make_async_copy(a, b, local.at[i])
        for i, (a, b) in enumerate(
            (
                (aper.at[0], aper_s),
                (src, src_s),
                (rec.at[0], rec_s),
                (traces.at[0], raw),
                (time_hbm, times),
                (amp_hbm, amps),
                (width_hbm, widths),
            )
        )
    ]
    barrier = pltpu.get_barrier_semaphore()
    for k in range(1, tiles):
        pl.semaphore_signal(
            barrier, inc=1, device_id={"tile": lax.rem(me + k, tiles)}, device_id_type=MESH
        )
    for load in loads:
        load.start()
    for k in range(1, classes):
        pl.semaphore_signal(
            barrier, inc=1, device_id={"offs": lax.rem(column + k, classes)}, device_id_type=MESH
        )

    weights[...] = band()
    image[...] = jnp.zeros_like(image)
    spread[...] = jnp.zeros_like(spread)
    own[:, :, pl.ds(ROWS - 8, 8), :] = jnp.zeros((blocks, pair, 8, LANES), jnp.float32)
    for load in loads[:4]:
        load.wait()

    def lay(b, carry):
        for c in range(samples // LANES):
            own[b, :, c, :] = raw[b, :, pl.ds(c * LANES, LANES)]
        rest = samples % LANES
        if rest:
            own[b, :, samples // LANES, pl.ds(0, rest)] = raw[b, :, pl.ds(samples - rest, rest)]
        return carry

    lax.fori_loop(0, blocks, lay, 0)
    lane = lax.broadcasted_iota(jnp.int32, (1, LANES), 1)

    def pack(k, carry):
        peer = lax.rem(me + k, tiles)
        first, second, named = jnp.int32(0), jnp.int32(0), jnp.int32(0)
        for b in range(blocks):
            hit = (aper_s[0, b] == peer) | (aper_s[1, b] == peer)
            first = jnp.where(hit & (named == 0), b, first)
            second = jnp.where(hit & (named == 1), b, second)
            named = named + hit.astype(jnp.int32)
        line = jnp.zeros((1, LANES), jnp.int32)
        for s, b in enumerate((first, second)):
            send[k, s] = own[b]
            line = jnp.where(lane == 4 * s, (named > s).astype(jnp.int32), line)
            line = jnp.where(lane == 4 * s + 1, src_s[0, b], line)
            line = jnp.where(lane == 4 * s + 2, rec_s[0, b], line)
            line = jnp.where(lane == 4 * s + 3, rec_s[1, b], line)
        note[pl.ds(k, 1)] = line
        return carry

    lax.fori_loop(0, tiles, pack, 0)
    notes[pl.ds(0, 1)] = note[pl.ds(0, 1)]
    recv[0] = send[0]

    def note_copy(k):
        return pltpu.make_async_remote_copy(
            note.at[pl.ds(k, 1)], notes.at[pl.ds(k, 1)], note_send, note_recv,
            device_id={"tile": lax.rem(me + k, tiles)}, device_id_type=MESH,
        )

    def trace_copy(k):
        return pltpu.make_async_remote_copy(
            send.at[k], recv.at[k], send_sem.at[k], recv_sem.at[k],
            device_id={"tile": lax.rem(me + k, tiles)}, device_id_type=MESH,
        )

    def each(first, last, action):
        def step(k, carry):
            action(k)
            return carry

        lax.fori_loop(first, last, step, 0)

    def turn(j):
        k = jnp.int32(0)
        for place, offset in enumerate(ORDER, 1):
            k = jnp.where(j == place, offset, k)
        return k

    def send_turn(j):
        k = turn(j)
        return jnp.where(me % 2 == 0, k, tiles - k)

    def recv_turn(j):
        k = turn(j)
        return jnp.where((me + k) % 2 == 0, k, tiles - k)

    pl.semaphore_wait(barrier, tiles + classes - 2)
    each(1, tiles, lambda k: note_copy(k).start())
    each(1, tiles, lambda j: trace_copy(send_turn(j)).start())
    for load in loads[4:]:
        load.wait()
    others = pl.ds(0, tiles - 1)
    pltpu.make_async_copy(notes.at[others], notes.at[others], note_recv).wait()
    to_scalar = pltpu.make_async_copy(notes, notes_s, local.at[len(loads)])
    to_scalar.start()
    to_scalar.wait()
    pltpu.make_async_copy(note.at[others], note.at[others], note_send).wait()
    wide = lax.broadcasted_iota(jnp.int32, (ROWS, LANES), 1)
    deep = lax.broadcasted_iota(jnp.int32, (ROWS, LANES), 0)
    eight = lax.broadcasted_iota(jnp.int32, (8, LANES), 0)
    ends = jnp.where(deep < 2 * REACH, deep - 2 * REACH, 4 * LANES)
    ends = jnp.where(deep < REACH, deep + LANES, ends)
    spots = [deep + ROWS * n for n in range(LANES // ROWS)] + [ends]
    spots = [x.astype(jnp.float32).astype(SPLIT) for x in spots]
    none = jnp.zeros((ROWS, LANES), SPLIT)

    def source(k, ready):
        jobs = []
        for s in range(2):
            live = notes_s[k, 4 * s] > 0
            node = notes_s[k, 4 * s + 1]
            source_time, source_amp, source_width = times[node], amps[node], widths[node]
            for i in range(pair):
                node = notes_s[k, 4 * s + 2 + i]
                sample = source_time + times[node]
                weight = jnp.where(live, source_amp * amps[node], 0.0)
                jobs.append((sample, weight, jnp.maximum(source_width, widths[node])))

        def prepare(n):
            sample, weight, width = jobs[n]
            tops = [h + 1 for h in HALF_WIDTHS]
            top = jnp.where(width == 0, tops[0], jnp.where(width == 1, tops[1], tops[2]))
            scale = jnp.where(
                width == 0,
                1.0 / tops[0] ** 2,
                jnp.where(width == 1, 1.0 / tops[1] ** 2, 1.0 / tops[2] ** 2),
            )
            m = n - GATHERED
            lines[m, 0] = (sample & (LANES - 1)).astype(jnp.float32)
            lines[m, 1] = top.astype(jnp.float32)
            lines[m, 2] = weight * scale
            rows[m] = sample >> 7

        for n in range(GATHERED, 2 * pair):
            prepare(n)
        ready()
        parts = []
        for s in range(2):
            for i in range(pair):
                x = recv[k, s, i]
                edge = jnp.where(
                    wide < REACH,
                    pltpu.roll(x, ROWS - 1, 0),
                    pltpu.roll(pltpu.roll(x, 1, 0), 2 * REACH, 1),
                )[:, :EDGE]
                xs, es = halves(x), halves(edge)
                parts += [jnp.concatenate([a, b], 1) for a, b in zip(xs, es)]
        total = jnp.dot(
            jnp.concatenate(parts[: 2 * GATHERED], 0),
            weights[...],
            preferred_element_type=jnp.float32,
        )
        for n in range(GATHERED):
            for c, h in enumerate(HALF_WIDTHS):
                lanes = slice(c * LANES, (c + 1) * LANES)
                high = total[2 * n * ROWS : (2 * n + 1) * ROWS, lanes]
                low = total[(2 * n + 1) * ROWS : (2 * n + 2) * ROWS, lanes]
                filtered[n, pl.ds(c * ROWS, ROWS)] = (high + low) * (1.0 / (h + 1) ** 2)
        sums = [jnp.zeros((8, LANES), jnp.float32) for _ in range(DEPTH // 8)]

        def gather(n, z):
            sample, weight, width = jobs[n]
            row = width * ROWS + (sample >> 7)
            place = sample & (LANES - 1)
            cut = slice(8 * z, 8 * z + 8)
            picked = jnp.zeros((8, LANES), jnp.float32)
            for r in range(CLASSES * ROWS):
                values = jnp.broadcast_to(filtered[n, pl.ds(r, 1)], (8, LANES))
                values = jnp.take_along_axis(
                    values, place[cut], axis=1, mode="promise_in_bounds"
                )
                picked = jnp.where(row[cut] == r, values, picked)
            sums[z] += weight[cut] * picked

        def product(n, zs):
            m = n - GATHERED
            cols = []
            for z in zs:
                at = jnp.broadcast_to(lines[m, 0, pl.ds(z, 1)], (ROWS, LANES)).astype(SPLIT)
                top = jnp.broadcast_to(lines[m, 1, pl.ds(z, 1)], (ROWS, LANES)).astype(SPLIT)
                cols.append(
                    jnp.concatenate([jnp.maximum(top - jnp.abs(x - at), none) for x in spots], 0)
                )
            got = jnp.dot(
                jnp.concatenate(parts[2 * n : 2 * n + 2], 0),
                jnp.concatenate(cols, 1),
                preferred_element_type=jnp.float32,
            )
            got = got[:ROWS] + got[ROWS:]
            for q, z in enumerate(zs):
                lanes = slice(q * LANES, (q + 1) * LANES)
                row = jnp.broadcast_to(rows[m, pl.ds(z, 1)], (8, LANES)) - eight
                picked = jnp.where(row == 0, got[:8, lanes], 0.0)
                picked = jnp.where(row == 8, got[8:, lanes], picked)
                spread[z] += picked * jnp.broadcast_to(lines[m, 2, pl.ds(z, 1)], (8, LANES))

        products = [(n, (z, z + 1)) for n in range(GATHERED, 2 * pair) for z in range(0, DEPTH, 2)]
        gathers = [(n, z) for n in range(GATHERED) for z in range(DEPTH // 8)]
        total_steps = max(len(products), len(gathers))
        for step in range(total_steps):
            for g in range(step * len(gathers) // total_steps, (step + 1) * len(gathers) // total_steps):
                gather(*gathers[g])
            for p in range(step * len(products) // total_steps, (step + 1) * len(products) // total_steps):
                product(*products[p])
        image[...] += jnp.concatenate(sums, 0)

    source(jnp.int32(0), lambda: None)

    def arrive(j, carry):
        k = recv_turn(j)
        source(k, trace_copy(k).wait_recv)
        trace_copy(k).wait_send()
        return carry

    lax.fori_loop(1, tiles, arrive, 0)
    image[...] += jnp.sum(spread[...], axis=1)

    def row_copy(k):
        to = lax.rem(column + k, classes)
        return pltpu.make_async_remote_copy(
            image.at[pl.ds(to, 1)], out.at[pl.ds(column, 1)], row_send, row_recv,
            device_id={"offs": to}, device_id_type=MESH,
        )

    for k in range(1, classes):
        row_copy(k).start()
    mine = pltpu.make_async_copy(
        image.at[pl.ds(column, 1)], out.at[pl.ds(column, 1)], local.at[len(loads)]
    )
    mine.start()
    mine.wait()
    rest = pl.ds(0, classes - 1)
    pltpu.make_async_copy(image.at[rest], image.at[rest], row_send).wait()
    pltpu.make_async_copy(image.at[rest], image.at[rest], row_recv).wait()


def body(traces, src_node, rec_node, aperture, time_table, amp_table, width_table):
    tiles = lax.axis_size("tile")
    classes = lax.axis_size("offs")
    _, blocks, pair, samples = traces.shape
    nodes = time_table.shape[0]
    tables = [t.reshape(nodes, DEPTH, CELLS) for t in (time_table, amp_table, width_table)]
    f32, i32 = jnp.float32, jnp.int32
    dma = pltpu.SemaphoreType.DMA
    slab = pl.pallas_call(
        migrate,
        out_shape=jax.ShapeDtypeStruct((classes, CELLS), f32),
        in_specs=[pl.BlockSpec(memory_space=pl.ANY)] * 7,
        out_specs=pl.BlockSpec(memory_space=pl.ANY),
        scratch_shapes=[
            pltpu.VMEM((blocks, pair, samples), f32),
            pltpu.VMEM((blocks, pair, ROWS, LANES), f32),
            pltpu.VMEM((tiles, 2, pair, ROWS, LANES), f32),
            pltpu.VMEM((tiles, 2, pair, ROWS, LANES), f32),
            pltpu.VMEM((tiles, LANES), i32),
            pltpu.VMEM((tiles, LANES), i32),
            pltpu.SMEM((tiles, LANES), i32),
            pltpu.SMEM((1, blocks), i32),
            pltpu.SMEM((pair, blocks), i32),
            pltpu.SMEM((2, blocks), i32),
            pltpu.VMEM((nodes, DEPTH, CELLS), i32),
            pltpu.VMEM((nodes, DEPTH, CELLS), f32),
            pltpu.VMEM((nodes, DEPTH, CELLS), i32),
            pltpu.VMEM((LANES + EDGE, CLASSES * LANES), SPLIT),
            pltpu.VMEM((2 * pair, CLASSES * ROWS, LANES), f32),
            pltpu.VMEM((DEPTH, CELLS), f32),
            pltpu.VMEM((DEPTH, 8, CELLS), f32),
            pltpu.VMEM((4, 3, DEPTH, CELLS), f32),
            pltpu.VMEM((4, DEPTH, CELLS), i32),
            dma((8,)),
            dma((tiles,)),
            dma((tiles,)),
            dma,
            dma,
            dma,
            dma,
        ],
        compiler_params=pltpu.CompilerParams(collective_id=0, has_side_effects=True),
        name="migrate",
    )(traces, src_node, jnp.swapaxes(rec_node, 1, 2), jnp.swapaxes(aperture, 1, 2), *tables)
    return slab[None, None]


def solution(mesh):
    return jax.shard_map(
        body,
        mesh=mesh,
        in_specs=(
            P("offs", "tile", None, None),
            P("offs", "tile"),
            P("offs", "tile", None),
            P("offs", "tile", None),
            P(None, "tile", None),
            P(None, "tile", None),
            P(None, "tile", None),
        ),
        out_specs=P("tile", "offs", None, None),
        check_vma=False,
    )
```

```python
import jax
import jax.numpy as jnp
from jax import lax
from jax.experimental import pallas as pl
from jax.experimental.pallas import tpu as pltpu
from jax.sharding import PartitionSpec as P

CELLS = 128
DEPTH = 16
ROWS = 16
LANES = 128
SPLIT = jnp.bfloat16
HALF_WIDTHS = (1, 2, 4)
CLASSES = len(HALF_WIDTHS)
EDGE = 16
REACH = 4
GATHERED = 1
MESH = pl.DeviceIdType.MESH
ORDER = (1, 2, 14, 8, 4, 12, 15, 3, 13, 6, 10, 7, 5, 11, 9)


def band():
    depth = LANES + EDGE
    k = lax.broadcasted_iota(jnp.int32, (depth, CLASSES * LANES), 0)
    column = lax.broadcasted_iota(jnp.int32, (depth, CLASSES * LANES), 1)
    far = jnp.where(k < LANES + 2 * REACH, k - LANES - 2 * REACH, 4 * LANES)
    place = jnp.where(k < LANES + REACH, k, far)
    apart = jnp.abs(place - (column & (LANES - 1)))
    top = jnp.where(column < LANES, HALF_WIDTHS[0] + 1, HALF_WIDTHS[1] + 1)
    top = jnp.where(column < 2 * LANES, top, HALF_WIDTHS[2] + 1)
    return jnp.maximum(top - apart, 0).astype(jnp.float32).astype(SPLIT)


def halves(x):
    high = x.astype(SPLIT)
    return high, (x - high.astype(jnp.float32)).astype(SPLIT)


def migrate(
    traces, src, rec, aper, time_hbm, amp_hbm, width_hbm, out,
    raw, own, send, recv, note, notes, notes_s, src_s, rec_s, aper_s,
    times, amps, widths, weights, filtered, image, spread, lines, rows,
    local, send_sem, recv_sem, note_send, note_recv, row_send, row_recv,
):
    me = lax.axis_index("tile")
    column = lax.axis_index("offs")
    tiles = recv.shape[0]
    classes = out.shape[0]
    blocks, pair = own.shape[0], own.shape[1]
    samples = raw.shape[2]
    loads = [
        pltpu.make_async_copy(a, b, local.at[i])
        for i, (a, b) in enumerate(
            (
                (aper.at[0], aper_s),
                (src, src_s),
                (rec.at[0], rec_s),
                (traces.at[0], raw),
                (time_hbm, times),
                (amp_hbm, amps),
                (width_hbm, widths),
            )
        )
    ]
    barrier = pltpu.get_barrier_semaphore()
    for k in range(1, tiles):
        pl.semaphore_signal(
            barrier, inc=1, device_id={"tile": lax.rem(me + k, tiles)}, device_id_type=MESH
        )
    for load in loads:
        load.start()
    for k in range(1, classes):
        pl.semaphore_signal(
            barrier, inc=1, device_id={"offs": lax.rem(column + k, classes)}, device_id_type=MESH
        )

    weights[...] = band()
    image[...] = jnp.zeros_like(image)
    spread[...] = jnp.zeros_like(spread)
    own[:, :, pl.ds(ROWS - 8, 8), :] = jnp.zeros((blocks, pair, 8, LANES), jnp.float32)
    for load in loads[:4]:
        load.wait()

    def lay(b, carry):
        for c in range(samples // LANES):
            own[b, :, c, :] = raw[b, :, pl.ds(c * LANES, LANES)]
        rest = samples % LANES
        if rest:
            own[b, :, samples // LANES, pl.ds(0, rest)] = raw[b, :, pl.ds(samples - rest, rest)]
        return carry

    lax.fori_loop(0, blocks, lay, 0)
    lane = lax.broadcasted_iota(jnp.int32, (1, LANES), 1)

    def pack(k, carry):
        peer = lax.rem(me + k, tiles)
        first, second, named = jnp.int32(0), jnp.int32(0), jnp.int32(0)
        for b in range(blocks):
            hit = (aper_s[0, b] == peer) | (aper_s[1, b] == peer)
            first = jnp.where(hit & (named == 0), b, first)
            second = jnp.where(hit & (named == 1), b, second)
            named = named + hit.astype(jnp.int32)
        line = jnp.zeros((1, LANES), jnp.int32)
        for s, b in enumerate((first, second)):
            send[k, s] = own[b]
            line = jnp.where(lane == 4 * s, (named > s).astype(jnp.int32), line)
            line = jnp.where(lane == 4 * s + 1, src_s[0, b], line)
            line = jnp.where(lane == 4 * s + 2, rec_s[0, b], line)
            line = jnp.where(lane == 4 * s + 3, rec_s[1, b], line)
        note[pl.ds(k, 1)] = line
        return carry

    lax.fori_loop(0, tiles, pack, 0)
    notes[pl.ds(0, 1)] = note[pl.ds(0, 1)]
    recv[0] = send[0]

    def note_copy(k):
        return pltpu.make_async_remote_copy(
            note.at[pl.ds(k, 1)], notes.at[pl.ds(k, 1)], note_send, note_recv,
            device_id={"tile": lax.rem(me + k, tiles)}, device_id_type=MESH,
        )

    def trace_copy(k):
        return pltpu.make_async_remote_copy(
            send.at[k], recv.at[k], send_sem.at[k], recv_sem.at[k],
            device_id={"tile": lax.rem(me + k, tiles)}, device_id_type=MESH,
        )

    def each(first, last, action):
        def step(k, carry):
            action(k)
            return carry

        lax.fori_loop(first, last, step, 0)

    def turn(j):
        k = jnp.int32(0)
        for place, offset in enumerate(ORDER, 1):
            k = jnp.where(j == place, offset, k)
        return k

    def send_turn(j):
        k = turn(j)
        return jnp.where(me % 2 == 0, k, tiles - k)

    def recv_turn(j):
        k = turn(j)
        return jnp.where((me + k) % 2 == 0, k, tiles - k)

    pl.semaphore_wait(barrier, tiles + classes - 2)
    each(1, tiles, lambda k: note_copy(k).start())
    each(1, tiles, lambda j: trace_copy(send_turn(j)).start())
    for load in loads[4:]:
        load.wait()
    others = pl.ds(0, tiles - 1)
    pltpu.make_async_copy(notes.at[others], notes.at[others], note_recv).wait()
    to_scalar = pltpu.make_async_copy(notes, notes_s, local.at[len(loads)])
    to_scalar.start()
    to_scalar.wait()
    pltpu.make_async_copy(note.at[others], note.at[others], note_send).wait()
    wide = lax.broadcasted_iota(jnp.int32, (ROWS, LANES), 1)
    deep = lax.broadcasted_iota(jnp.int32, (ROWS, LANES), 0)
    eight = lax.broadcasted_iota(jnp.int32, (8, LANES), 0)
    ends = jnp.where(deep < 2 * REACH, deep - 2 * REACH, 4 * LANES)
    ends = jnp.where(deep < REACH, deep + LANES, ends)
    spots = [deep + ROWS * n for n in range(LANES // ROWS)] + [ends]
    spots = [x.astype(jnp.float32).astype(SPLIT) for x in spots]
    none = jnp.zeros((ROWS, LANES), SPLIT)

    def source(k, ready):
        jobs = []
        for s in range(2):
            live = notes_s[k, 4 * s] > 0
            node = notes_s[k, 4 * s + 1]
            source_time, source_amp, source_width = times[node], amps[node], widths[node]
            for i in range(pair):
                node = notes_s[k, 4 * s + 2 + i]
                sample = source_time + times[node]
                weight = jnp.where(live, source_amp * amps[node], 0.0)
                jobs.append((sample, weight, jnp.maximum(source_width, widths[node])))

        def prepare(n):
            sample, weight, width = jobs[n]
            tops = [h + 1 for h in HALF_WIDTHS]
            top = jnp.where(width == 0, tops[0], jnp.where(width == 1, tops[1], tops[2]))
            scale = jnp.where(
                width == 0,
                1.0 / tops[0] ** 2,
                jnp.where(width == 1, 1.0 / tops[1] ** 2, 1.0 / tops[2] ** 2),
            )
            m = n - GATHERED
            lines[m, 0] = (sample & (LANES - 1)).astype(jnp.float32)
            lines[m, 1] = top.astype(jnp.float32)
            lines[m, 2] = weight * scale
            rows[m] = sample >> 7

        for n in range(GATHERED, 2 * pair):
            prepare(n)
        ready()
        parts = []
        for s in range(2):
            for i in range(pair):
                x = recv[k, s, i]
                edge = jnp.where(
                    wide < REACH,
                    pltpu.roll(x, ROWS - 1, 0),
                    pltpu.roll(pltpu.roll(x, 1, 0), 2 * REACH, 1),
                )[:, :EDGE]
                xs, es = halves(x), halves(edge)
                parts += [jnp.concatenate([a, b], 1) for a, b in zip(xs, es)]
        total = jnp.dot(
            jnp.concatenate(parts[: 2 * GATHERED], 0),
            weights[...],
            preferred_element_type=jnp.float32,
        )
        for n in range(GATHERED):
            for c, h in enumerate(HALF_WIDTHS):
                lanes = slice(c * LANES, (c + 1) * LANES)
                high = total[2 * n * ROWS : (2 * n + 1) * ROWS, lanes]
                low = total[(2 * n + 1) * ROWS : (2 * n + 2) * ROWS, lanes]
                filtered[n, pl.ds(c * ROWS, ROWS)] = (high + low) * (1.0 / (h + 1) ** 2)
        sums = [jnp.zeros((8, LANES), jnp.float32) for _ in range(DEPTH // 8)]

        def gather(n, z):
            sample, weight, width = jobs[n]
            row = width * ROWS + (sample >> 7)
            place = sample & (LANES - 1)
            cut = slice(8 * z, 8 * z + 8)
            picked = jnp.zeros((8, LANES), jnp.float32)
            for r in range(CLASSES * ROWS):
                values = jnp.broadcast_to(filtered[n, pl.ds(r, 1)], (8, LANES))
                values = jnp.take_along_axis(
                    values, place[cut], axis=1, mode="promise_in_bounds"
                )
                picked = jnp.where(row[cut] == r, values, picked)
            sums[z] += weight[cut] * picked

        def product(n, zs):
            m = n - GATHERED
            cols = []
            for z in zs:
                at = jnp.broadcast_to(lines[m, 0, pl.ds(z, 1)], (ROWS, LANES)).astype(SPLIT)
                top = jnp.broadcast_to(lines[m, 1, pl.ds(z, 1)], (ROWS, LANES)).astype(SPLIT)
                cols.append(
                    jnp.concatenate([jnp.maximum(top - jnp.abs(x - at), none) for x in spots], 0)
                )
            got = jnp.dot(
                jnp.concatenate(parts[2 * n : 2 * n + 2], 0),
                jnp.concatenate(cols, 1),
                preferred_element_type=jnp.float32,
            )
            got = got[:ROWS] + got[ROWS:]
            for q, z in enumerate(zs):
                lanes = slice(q * LANES, (q + 1) * LANES)
                row = jnp.broadcast_to(rows[m, pl.ds(z, 1)], (8, LANES)) - eight
                picked = jnp.where(row == 0, got[:8, lanes], 0.0)
                picked = jnp.where(row == 8, got[8:, lanes], picked)
                spread[z] += picked * jnp.broadcast_to(lines[m, 2, pl.ds(z, 1)], (8, LANES))

        products = [(n, (z, z + 1)) for n in range(GATHERED, 2 * pair) for z in range(0, DEPTH, 2)]
        gathers = [(n, z) for n in range(GATHERED) for z in range(DEPTH // 8)]
        total_steps = max(len(products), len(gathers))
        for step in range(total_steps):
            for g in range(step * len(gathers) // total_steps, (step + 1) * len(gathers) // total_steps):
                gather(*gathers[g])
            for p in range(step * len(products) // total_steps, (step + 1) * len(products) // total_steps):
                product(*products[p])
        image[...] += jnp.concatenate(sums, 0)

    source(jnp.int32(0), lambda: None)

    def arrive(j, carry):
        k = recv_turn(j)
        source(k, trace_copy(k).wait_recv)
        return carry

    lax.fori_loop(1, tiles, arrive, 0)
    image[...] += jnp.sum(spread[...], axis=1)

    def row_copy(k):
        to = lax.rem(column + k, classes)
        return pltpu.make_async_remote_copy(
            image.at[pl.ds(to, 1)], out.at[pl.ds(column, 1)], row_send, row_recv,
            device_id={"offs": to}, device_id_type=MESH,
        )

    for k in range(1, classes):
        row_copy(k).start()
    mine = pltpu.make_async_copy(
        image.at[pl.ds(column, 1)], out.at[pl.ds(column, 1)], local.at[len(loads)]
    )
    mine.start()
    mine.wait()
    each(1, tiles, lambda k: trace_copy(k).wait_send())
    rest = pl.ds(0, classes - 1)
    pltpu.make_async_copy(image.at[rest], image.at[rest], row_send).wait()
    pltpu.make_async_copy(image.at[rest], image.at[rest], row_recv).wait()


def body(traces, src_node, rec_node, aperture, time_table, amp_table, width_table):
    tiles = lax.axis_size("tile")
    classes = lax.axis_size("offs")
    _, blocks, pair, samples = traces.shape
    nodes = time_table.shape[0]
    tables = [t.reshape(nodes, DEPTH, CELLS) for t in (time_table, amp_table, width_table)]
    f32, i32 = jnp.float32, jnp.int32
    dma = pltpu.SemaphoreType.DMA
    slab = pl.pallas_call(
        migrate,
        out_shape=jax.ShapeDtypeStruct((classes, CELLS), f32),
        in_specs=[pl.BlockSpec(memory_space=pl.ANY)] * 7,
        out_specs=pl.BlockSpec(memory_space=pl.ANY),
        scratch_shapes=[
            pltpu.VMEM((blocks, pair, samples), f32),
            pltpu.VMEM((blocks, pair, ROWS, LANES), f32),
            pltpu.VMEM((tiles, 2, pair, ROWS, LANES), f32),
            pltpu.VMEM((tiles, 2, pair, ROWS, LANES), f32),
            pltpu.VMEM((tiles, LANES), i32),
            pltpu.VMEM((tiles, LANES), i32),
            pltpu.SMEM((tiles, LANES), i32),
            pltpu.SMEM((1, blocks), i32),
            pltpu.SMEM((pair, blocks), i32),
            pltpu.SMEM((2, blocks), i32),
            pltpu.VMEM((nodes, DEPTH, CELLS), i32),
            pltpu.VMEM((nodes, DEPTH, CELLS), f32),
            pltpu.VMEM((nodes, DEPTH, CELLS), i32),
            pltpu.VMEM((LANES + EDGE, CLASSES * LANES), SPLIT),
            pltpu.VMEM((2 * pair, CLASSES * ROWS, LANES), f32),
            pltpu.VMEM((DEPTH, CELLS), f32),
            pltpu.VMEM((DEPTH, 8, CELLS), f32),
            pltpu.VMEM((4, 3, DEPTH, CELLS), f32),
            pltpu.VMEM((4, DEPTH, CELLS), i32),
            dma((8,)),
            dma((tiles,)),
            dma((tiles,)),
            dma,
            dma,
            dma,
            dma,
        ],
        compiler_params=pltpu.CompilerParams(collective_id=0, has_side_effects=True),
        name="migrate",
    )(traces, src_node, jnp.swapaxes(rec_node, 1, 2), jnp.swapaxes(aperture, 1, 2), *tables)
    return slab[None, None]


def solution(mesh):
    return jax.shard_map(
        body,
        mesh=mesh,
        in_specs=(
            P("offs", "tile", None, None),
            P("offs", "tile"),
            P("offs", "tile", None),
            P("offs", "tile", None),
            P(None, "tile", None),
            P(None, "tile", None),
            P(None, "tile", None),
        ),
        out_specs=P("tile", "offs", None, None),
        check_vma=False,
    )
```
